32 devices in a mesh: ops: 16 (over z, y, x), blk: 2 (over core).
Axes of the slice: x: 2, y: 2, z: 4, core: 2. Of those that a mesh axis runs over, the one named last changes fastest.
Arguments:
- operators_left: bfloat16 [1024, 256, 256], P('ops', None, 'blk'), may hold values from -6 to 6
- operators_right: bfloat16 [1024, 256, 256], P('ops'), may hold values from -0.0007324219 to 0.0007324219
- wavefunction: bfloat16 [256, 3, 256], P('blk', None, 'ops'), may hold values from -6 to 6
- rotation: bfloat16 [256, 128], replicated, may hold values from -0.375 to 0.375
- pair_count: int32 [16], P('ops'), may hold values from 16 to 64, as said below
- next_owner: int32 [1024, 1], P('ops'), may hold values from 0 to 15; in each aligned block of 64 rows (0 to 63, 64 to 127, ...) at most 8 rows name the same one
Outputs:
- sigma: float32 [256, 3, 256], P(('ops', 'blk'))
- renewed: bfloat16 [16, 128, 128, 128], P('ops', None, 'blk')
The draws below stay inside these ranges and needn't reach their ends.
Inputs may be any that keep to these rules, and one draw needn't show every extreme that they name: Each owner's live pairs fill its first pair_count slots; at least one owner has all 64 slots live. `next_owner`: among the 64 slots of one owner, at most 8 name the same next owner.
All inputs are finite; a program needn't handle non-finite values.
Results may differ from the reference program's by a relative error of at most 0.0073.
Values may be sent and summed in bfloat16 or wider, within the bound.
A program may use at most 128 MiB of HBM per device.

```python
import math
import jax
import jax.numpy as jnp
import numpy as np
from jax import lax

L = 256
R = 256
K = 128
NV = 3
SLOTS = 64
PAIRS = 1024
CAP = 8
INBOX = 128
N_OPS = 16


def draw_pair_count(key, part):
    owners = PAIRS // SLOTS
    counts = jax.random.randint(jax.random.fold_in(key, 11), (owners,), SLOTS // 4, 3 * SLOTS // 4 + 1, dtype=jnp.int32)
    fullest = jax.random.randint(jax.random.fold_in(key, 12), (), 0, owners, dtype=jnp.int32)
    return jnp.where(jnp.arange(owners, dtype=jnp.int32) == fullest, SLOTS, counts).astype(jnp.int32)


def spiked(entries, stream_key, source, target, blocks, factor):
    owner, partner = [(jnp.arange(entries.shape[axis_at]) // (entries.shape[axis_at] // blocks)).reshape([-1 if axis == axis_at else 1 for axis in range(entries.ndim)]) for axis_at in (source, target)]
    chosen = jax.random.permutation(stream_key, blocks)[partner]
    strong = (owner == chosen) | (owner == (partner + blocks // 2) % blocks)
    return jnp.where(strong, factor * entries, entries)


def steps_of(own_key, shape, shards, least, high):
    loudness, own = 1.0, jax.random.fold_in(own_key, 6)
    for position, blocks in shards:
        heights = jnp.exp(jax.random.uniform(jax.random.fold_in(own, position), (blocks,), jnp.float32, least / len(shards), high / len(shards)))
        loudness = loudness * jnp.repeat(heights, shape[position] // blocks).reshape([-1 if axis == position else 1 for axis in range(len(shape))])
    return loudness


def routed_block(own_key, own, number, rows, amount, top, reach, slope):
    order = jax.random.permutation(own_key, amount)
    crowded, common = load_shares(amount, rows * top, reach, slope, True), load_shares(amount, rows * top, reach, slope, False)
    places = jnp.arange(amount)

    def named(tallies, offset_by):
        used = int((tallies > 0).sum())
        fixed = max(1, used // 4)
        passed = fixed + (places - fixed + offset_by * (used - fixed)) % max(1, amount - fixed)
        return jnp.zeros((amount,), jnp.int32).at[order[jnp.where(places < fixed, places, passed)]].set(jnp.asarray(tallies, jnp.int32))

    tallies = jnp.where(number % 4 == 0, named(crowded, number // 4), named(common, number - number // 4 - 1))
    mixed = jax.random.permutation(jax.random.fold_in(own, 3), amount)
    source_of, receiver = mixed[0:amount // 2 * 2:2], mixed[1:amount // 2 * 2:2]
    room = jnp.minimum(tallies[source_of] - 1, reach - tallies[receiver]) // 2
    room = jnp.where((source_of == order[0]) | (receiver == order[0]) | (tallies[receiver] == 0), 0, jnp.maximum(room, 0))
    passed = jax.random.randint(jax.random.fold_in(own, 4), (amount // 2,), 0, 1 << 20) % (room + 1)
    tallies = tallies.at[source_of].add(-passed).at[receiver].add(passed)
    items = jnp.searchsorted(jnp.cumsum(tallies), jnp.arange(rows * top), side="right").astype(jnp.int32)
    grid = items.reshape(top, rows).T
    grid = grid[jax.random.permutation(jax.random.fold_in(own, 1), rows)]
    offset_by = jax.random.randint(jax.random.fold_in(own, 2), (rows, 1), 0, top)
    return jnp.take_along_axis(grid, (jnp.arange(top)[None, :] + offset_by) % top, axis=1)


def load_shares(amount, total, most, slope, full):
    weights = [(1 << 20) // math.isqrt(standing ** slope) + 1 for standing in range(1, amount + 1)]
    largest = most if full else min(most, max(-(-total // amount), total * weights[0] // sum(weights)))
    least = 1 if total - largest >= amount - 1 else 0
    given, spare = [largest] + [least] * (amount - 1), total - largest - least * (amount - 1)
    while spare > 0:
        free = [i for i in range(1, amount) if given[i] < largest] or [i for i in range(1, amount) if given[i] < most]
        pool, budget = sum([weights[i] for i in free]), spare
        for i in free:
            addition = min(most - given[i], max(1, budget * weights[i] // pool), spare)
            given[i] = given[i] + addition
            spare = spare - addition
    return np.array(given)


def centred(key, extent, scale, bound, shards=(), kind=jnp.bfloat16):
    drawn = jax.random.normal(key, extent, jnp.float32) * scale
    if len(shards) > 0:
        drawn = steps_of(key, extent, shards, -0.22, 0.18) * drawn
    return jnp.clip(drawn, min=-bound, max=bound).astype(kind)


def gaussian_with(own_key, dims, deviation, most, pieces, heavy, kind=jnp.bfloat16):
    array = deviation * jax.random.normal(own_key, dims, jnp.float32)
    if pieces:
        array = array * steps_of(own_key, dims, pieces, -0.22, 0.18)
    return jnp.clip(spiked(array, jax.random.fold_in(own_key, 3), *heavy), -most, most).astype(kind)


def setup_inputs(seed: int = 0) -> dict:
    key_of = jax.random.split(jax.random.key(seed), 7)
    operators_left = gaussian_with(key_of[0], (PAIRS, L, L), 1.0, 6.0, ((0, 16), (2, 2)), (0, 1, 16, 2.0))
    operators_right = centred(key_of[1], (PAIRS, R, R), (R * L * PAIRS) ** -0.5, 0.0007324219, ((0, 16),))
    wavefunction = centred(key_of[2], (L, NV, R), 1.0, 6.0, ((0, 2), (2, 16)))
    rotation = centred(key_of[3], (L, K), L ** -0.5, 0.375)
    pair_count = draw_pair_count(jax.random.fold_in(key_of[6], 71), 0)
    next_owner_keys = jax.random.split(jax.random.fold_in(key_of[5], 1), PAIRS // SLOTS)
    next_owner_turns = jax.random.permutation(jax.random.fold_in(key_of[5], 3), PAIRS // SLOTS)
    next_owner = jax.vmap(lambda own, number: routed_block(jax.random.fold_in(key_of[5], 2), own, number, SLOTS, N_OPS, 1, CAP, 2))(next_owner_keys, next_owner_turns).reshape((PAIRS, 1))
    return {"operators_left": operators_left, "operators_right": operators_right, "wavefunction": wavefunction, "rotation": rotation, "pair_count": pair_count, "next_owner": next_owner}


def reference(operators_left, operators_right, wavefunction, rotation, pair_count, next_owner):
    wave_float = wavefunction.astype(jnp.float32)
    rot_float = rotation.astype(jnp.float32)
    left_grouped = operators_left.reshape(N_OPS, SLOTS, L, L)
    right_grouped = operators_right.reshape(N_OPS, SLOTS, R, R)
    owner_targets = next_owner.reshape(N_OPS, SLOTS)

    def owner_work(packed):
        lefts, rights, live_count, targets = packed
        living = jnp.arange(SLOTS, dtype=jnp.int32) < live_count
        lefts_float = lefts.astype(jnp.float32)
        products = jnp.einsum("inr,psr->pins", wave_float, rights.astype(jnp.float32)).astype(jnp.bfloat16)
        products = jnp.where(living[:, None, None, None], products, jnp.zeros_like(products))
        term = jnp.einsum("pij,pjns->ins", lefts_float, products.astype(jnp.float32))
        rotated = jnp.einsum("ik,pij->pkj", rot_float, lefts_float).astype(jnp.bfloat16)
        blocks = jnp.einsum("pkj,jl->pkl", rotated.astype(jnp.float32), rot_float).astype(jnp.bfloat16)
        blocks = jnp.where(living[:, None, None], blocks, jnp.zeros_like(blocks))
        chosen = ((targets[:, None] == jnp.arange(N_OPS, dtype=jnp.int32)[None, :]) & living[:, None]).astype(jnp.int32)
        earlier = jnp.cumsum(chosen, axis=0) - chosen
        ranking = jnp.sum(earlier * chosen, axis=1)
        address = targets * CAP + ranking
        placing = ((address[None, :] == jnp.arange(N_OPS * CAP, dtype=jnp.int32)[:, None]) & living[None, :]).astype(jnp.float32)
        outgoing = jnp.einsum("ap,pkl->akl", placing, blocks.astype(jnp.float32)).astype(jnp.bfloat16)
        return term, outgoing

    terms, sent = lax.map(owner_work, (left_grouped, right_grouped, pair_count, owner_targets))
    sigma = jnp.sum(terms, axis=0)
    renewed = sent.reshape(N_OPS, N_OPS, CAP, K, K).transpose(1, 0, 2, 3, 4).reshape(N_OPS, INBOX, K, K)
    return sigma, renewed
```

```python
import functools

import jax
import jax.numpy as jnp
from jax import lax
from jax.experimental import pallas as pl
from jax.experimental.pallas import tpu as pltpu
from jax.sharding import PartitionSpec as P

MESH = pl.DeviceIdType.MESH
CHUNKS = 4
GROUP = 8


def kernel(
    n_ops,
    n_blk,
    inbox_ref,
    count_ref,
    left_hbm,
    right_hbm,
    wave_ref,
    rot_ref,
    sigma_ref,
    renewed_ref,
    left,
    right,
    rot_turned,
    rot_rows,
    rot_cols,
    w_mine,
    w_send,
    w_recv,
    blocks,
    outbox,
    wave_all,
    wave_full,
    z_group,
    total,
    sig_send,
    sig_recv,
    left_sem,
    right_sem,
    w_ssem,
    w_rsem,
    wave_ssem,
    wave_rsem,
    out_ssem,
    out_rsem,
    own_sem,
    sig_ssem,
    sig_rsem,
):
    ops = lax.axis_index("ops")
    blk = lax.axis_index("blk")
    me = ops * n_blk + blk
    n_all = n_ops * n_blk
    slots, left_states, half = left.shape
    right_states = right.shape[1]
    new_half = w_mine.shape[1]
    vectors = sigma_ref.shape[1]
    capacity = outbox.shape[0] // n_ops
    step = slots // CHUNKS

    def left_copy(c):
        at = pl.ds(c * step, step)
        return pltpu.make_async_copy(left_hbm.at[at], left.at[at], left_sem.at[c])

    def right_copy(c):
        at = pl.ds(c * step, step)
        return pltpu.make_async_copy(right_hbm.at[at], right.at[at], right_sem.at[c])

    for c in range(CHUNKS):
        left_copy(c).start()
    for c in range(CHUNKS):
        right_copy(c).start()

    barrier = pltpu.get_barrier_semaphore()

    def greet(s, carry):
        other = lax.rem(me + s, n_all)
        pl.semaphore_signal(
            barrier,
            inc=1,
            device_id={"ops": lax.div(other, n_blk), "blk": lax.rem(other, n_blk)},
            device_id_type=MESH,
        )
        return carry

    lax.fori_loop(1, n_all, greet, 0)

    def w_copy(c):
        at = pl.ds(c * step, step)
        return pltpu.make_async_remote_copy(
            src_ref=w_send.at[at],
            dst_ref=w_recv.at[at],
            send_sem=w_ssem.at[c],
            recv_sem=w_rsem.at[c],
            device_id={"ops": ops, "blk": 1 - blk},
            device_id_type=MESH,
        )

    def wave_copy(s):
        return pltpu.make_async_remote_copy(
            src_ref=wave_ref,
            dst_ref=wave_all.at[ops],
            send_sem=wave_ssem.at[s],
            recv_sem=wave_rsem.at[s],
            device_id={"ops": lax.rem(ops + s, n_ops), "blk": blk},
            device_id_type=MESH,
        )

    def out_copy(s):
        target = lax.rem(ops + s, n_ops)
        return pltpu.make_async_remote_copy(
            src_ref=outbox.at[pl.ds(target * capacity, capacity)],
            dst_ref=renewed_ref.at[0, pl.ds(ops * capacity, capacity)],
            send_sem=out_ssem.at[s],
            recv_sem=out_rsem.at[s],
            device_id={"ops": target, "blk": blk},
            device_id_type=MESH,
        )

    def sig_copy(s):
        other = lax.rem(me + s, n_all)
        return pltpu.make_async_remote_copy(
            src_ref=sig_send.at[other],
            dst_ref=sig_recv.at[me],
            send_sem=sig_ssem.at[s],
            recv_sem=sig_rsem.at[s],
            device_id={"ops": lax.div(other, n_blk), "blk": lax.rem(other, n_blk)},
            device_id_type=MESH,
        )

    rot_turned[...] = rot_ref[...].T
    rot_cols[pl.ds(0, new_half)] = rot_turned[pl.ds(blk * new_half, new_half)]
    rot_cols[pl.ds(new_half, new_half)] = rot_turned[pl.ds((1 - blk) * new_half, new_half)]
    rot_rows[pl.ds(0, half)] = rot_ref[pl.ds(blk * half, half)]
    rot_rows[pl.ds(half, half)] = rot_ref[pl.ds((1 - blk) * half, half)]

    def rotate(i, carry):
        p = 2 * i
        both = jnp.concatenate([left[p], left[p + 1]], axis=1)
        w = jnp.dot(rot_cols[...], both, preferred_element_type=jnp.float32)
        w = w.astype(jnp.bfloat16)
        w_mine[p] = w[:new_half, :half]
        w_mine[p + 1] = w[:new_half, half:]
        w_send[p] = w[new_half:, :half]
        w_send[p + 1] = w[new_half:, half:]
        return carry

    for c in range(CHUNKS):
        left_copy(c).wait()
        lax.fori_loop(c * step // 2, (c + 1) * step // 2, rotate, 0)
        if c == 0:
            pl.semaphore_wait(barrier, n_all - 1)
        else:
            w_copy(c - 1).start()

    def start_wave(s, carry):
        wave_copy(s).start()
        return carry

    lax.fori_loop(1, n_ops, start_wave, 0)
    wave_all[ops] = wave_ref[...]
    w_copy(CHUNKS - 1).start()

    blocks[slots] = jnp.zeros(blocks.shape[1:], blocks.dtype)
    part = 4

    def renew(i, carry):
        at = pl.ds(i * part, part)
        w = jnp.concatenate(
            [
                w_mine[at].reshape(part * new_half, half),
                w_recv[at].reshape(part * new_half, half),
            ],
            axis=1,
        )
        b = jnp.dot(w, rot_rows[...], preferred_element_type=jnp.float32)
        blocks[at] = b.astype(jnp.bfloat16).reshape(part, new_half, b.shape[1])
        return carry

    for c in range(CHUNKS):
        w_copy(c).wait()
        lax.fori_loop(c * step // part, (c + 1) * step // part, renew, 0)

    def fill(s):
        first = lax.rem(ops + s, n_ops) * capacity
        for a in range(capacity):
            outbox[first + a] = blocks[inbox_ref[first + a]]

    fill(1)

    def fill_and_send(s, carry):
        fill(s + 1)
        out_copy(s).start()
        return carry

    lax.fori_loop(1, n_ops, fill_and_send, 0)

    def wait_wave(s, carry):
        wave_copy(s).wait()
        return carry

    lax.fori_loop(1, n_ops, wait_wave, 0)
    padded = wave_all.shape[1]
    gathered = wave_all[...].reshape(n_ops * padded, wave_all.shape[2])
    columns = right_states // n_ops
    if padded == columns:
        wave_full[...] = gathered
    else:
        row = lax.broadcasted_iota(jnp.int32, (right_states, n_ops * padded), 0)
        col = lax.broadcasted_iota(jnp.int32, (right_states, n_ops * padded), 1)
        pick = (row // columns) * padded + row % columns == col
        wave_full[...] = jnp.dot(
            pick.astype(jnp.bfloat16), gathered, preferred_element_type=jnp.float32
        ).astype(jnp.bfloat16)

    own = pltpu.make_async_copy(
        outbox.at[pl.ds(ops * capacity, capacity)],
        renewed_ref.at[0, pl.ds(ops * capacity, capacity)],
        own_sem,
    )
    own.start()

    total[...] = jnp.zeros_like(total)

    def apply(g, carry):
        for q in range(GROUP):
            p = g * GROUP + q
            scale = jnp.where(p < count_ref[0], 1.0, 0.0).astype(jnp.float32)
            z = jnp.dot(right[p], wave_full[...], preferred_element_type=jnp.float32)
            z = (z * scale).astype(jnp.bfloat16)
            for n in range(vectors):
                z_group[pl.ds(n * right_states, right_states), pl.ds(q * half, half)] = z[
                    :, n * half : (n + 1) * half
                ]
        lefts = jnp.concatenate([left[g * GROUP + q] for q in range(GROUP)], axis=1)
        for n in range(vectors):
            at = pl.ds(n * right_states, right_states)
            total[at] += lax.dot_general(
                z_group[at],
                lefts,
                (((1,), (1,)), ((), ())),
                preferred_element_type=jnp.float32,
            )
        return carry

    for c in range(CHUNKS):
        right_copy(c).wait()
        lax.fori_loop(c * step // GROUP, (c + 1) * step // GROUP, apply, 0)

    rows = sigma_ref.shape[0]
    for n in range(vectors):
        turned = total[pl.ds(n * right_states, right_states)].T
        sig_send[:, :, pl.ds(n * right_states, right_states)] = turned.reshape(
            n_all, rows, right_states
        ).astype(jnp.bfloat16)
    sig_recv[me] = sig_send[me]

    def start_sig(s, carry):
        sig_copy(s).start()
        return carry

    lax.fori_loop(1, n_all, start_sig, 0)

    def wait_sig(s, carry):
        sig_copy(s).wait()
        return carry

    lax.fori_loop(1, n_all, wait_sig, 0)
    summed = jnp.sum(sig_recv[...].astype(jnp.float32), axis=0)
    for n in range(vectors):
        sigma_ref[:, n, :] = summed[:, n * right_states : (n + 1) * right_states]

    def wait_out(s, carry):
        out_copy(s).wait()
        return carry

    lax.fori_loop(1, n_ops, wait_out, 0)
    own.wait()


def per_device(operators_left, operators_right, wavefunction, rotation, pair_count, next_owner):
    n_ops = lax.axis_size("ops")
    n_blk = lax.axis_size("blk")
    slots, left_states, half = operators_left.shape
    right_states = operators_right.shape[1]
    _, vectors, columns = wavefunction.shape
    new_states = rotation.shape[1]
    new_half = new_states // n_blk
    capacity = max(2, 2 * slots // n_ops)
    n_all = n_ops * n_blk
    rows = left_states // n_all

    targets = next_owner[:, 0]
    number = lax.iota(jnp.int32, slots)
    living = number < pair_count[0]
    same = (targets[:, None] == targets[None, :]) & (number[None, :] < number[:, None])
    ranking = jnp.sum((same & living[None, :]).astype(jnp.int32), axis=1)
    address = jnp.where(living, targets * capacity + ranking, -1)
    hit = address[None, :] == lax.iota(jnp.int32, n_ops * capacity)[:, None]
    source = jnp.min(jnp.where(hit, number[None, :], slots), axis=1)

    padded = -(-columns // 16) * 16
    wave = wavefunction.transpose(2, 1, 0).reshape(columns, vectors * half)
    wave = jnp.pad(wave, ((0, padded - columns), (0, 0)))

    bf16 = jnp.bfloat16
    dma = pltpu.SemaphoreType.DMA
    vmem = pl.BlockSpec(memory_space=pltpu.VMEM)
    smem = pl.BlockSpec(memory_space=pltpu.SMEM)
    anywhere = pl.BlockSpec(memory_space=pl.ANY)
    return pl.pallas_call(
        functools.partial(kernel, n_ops, n_blk),
        out_shape=(
            jax.ShapeDtypeStruct((rows, vectors, right_states), jnp.float32),
            jax.ShapeDtypeStruct((1, n_ops * capacity, new_half, new_states), bf16),
        ),
        in_specs=[smem, smem, anywhere, anywhere, vmem, vmem],
        out_specs=(vmem, anywhere),
        scratch_shapes=[
            pltpu.VMEM((slots, left_states, half), bf16),
            pltpu.VMEM((slots, right_states, right_states), bf16),
            pltpu.VMEM((new_states, left_states), bf16),
            pltpu.VMEM((left_states, new_states), bf16),
            pltpu.VMEM((new_states, left_states), bf16),
            pltpu.VMEM((slots, new_half, half), bf16),
            pltpu.VMEM((slots, new_half, half), bf16),
            pltpu.VMEM((slots, new_half, half), bf16),
            pltpu.VMEM((slots + 1, new_half, new_states), bf16),
            pltpu.VMEM((n_ops * capacity, new_half, new_states), bf16),
            pltpu.VMEM((n_ops, padded, vectors * half), bf16),
            pltpu.VMEM((right_states, vectors * half), bf16),
            pltpu.VMEM((vectors * right_states, GROUP * half), bf16),
            pltpu.VMEM((vectors * right_states, left_states), jnp.float32),
            pltpu.VMEM((n_all, rows, vectors * right_states), bf16),
            pltpu.VMEM((n_all, rows, vectors * right_states), bf16),
            dma((CHUNKS,)),
            dma((CHUNKS,)),
            dma((CHUNKS,)),
            dma((CHUNKS,)),
            dma((n_ops,)),
            dma((n_ops,)),
            dma((n_ops,)),
            dma((n_ops,)),
            dma(()),
            dma((n_all,)),
            dma((n_all,)),
        ],
        compiler_params=pltpu.CompilerParams(collective_id=0, has_side_effects=True),
        name="davidson_step",
    )(source, pair_count, operators_left, operators_right, wave, rotation)


def solution(mesh):
    in_specs = (
        P("ops", None, "blk"),
        P("ops", None, None),
        P("blk", None, "ops"),
        P(),
        P("ops"),
        P("ops", None),
    )
    out_specs = (P(("ops", "blk"), None, None), P("ops", None, "blk", None))
    return jax.shard_map(
        per_device, mesh=mesh, in_specs=in_specs, out_specs=out_specs, check_vma=False
    )
```

```python
import functools

import jax
import jax.numpy as jnp
from jax import lax
from jax.experimental import pallas as pl
from jax.experimental.pallas import tpu as pltpu
from jax.sharding import PartitionSpec as P

MESH = pl.DeviceIdType.MESH
CHUNKS = 4
GROUP = 8


def kernel(
    n_ops,
    n_blk,
    inbox_ref,
    count_ref,
    left_hbm,
    right_hbm,
    wave_ref,
    rot_ref,
    sigma_ref,
    renewed_ref,
    left,
    right,
    rot_turned,
    rot_rows,
    rot_cols,
    w_mine,
    w_send,
    w_recv,
    blocks,
    outbox,
    wave_all,
    wave_full,
    z_group,
    total,
    sig_send,
    sig_recv,
    mid_send,
    mid_recv,
    left_sem,
    right_sem,
    w_ssem,
    w_rsem,
    wave_ssem,
    wave_rsem,
    out_ssem,
    out_rsem,
    own_sem,
    sig_ssem,
    sig_rsem,
    mid_ssem,
    mid_rsem,
):
    ops = lax.axis_index("ops")
    blk = lax.axis_index("blk")
    me = ops * n_blk + blk
    n_all = n_ops * n_blk
    slots, left_states, half = left.shape
    right_states = right.shape[1]
    new_half = w_mine.shape[1]
    vectors = sigma_ref.shape[1]
    capacity = outbox.shape[0] // n_ops
    step = slots // CHUNKS

    def left_copy(c):
        at = pl.ds(c * step, step)
        return pltpu.make_async_copy(left_hbm.at[at], left.at[at], left_sem.at[c])

    def right_copy(c):
        at = pl.ds(c * step, step)
        return pltpu.make_async_copy(right_hbm.at[at], right.at[at], right_sem.at[c])

    for c in range(CHUNKS):
        left_copy(c).start()
    barrier = pltpu.get_barrier_semaphore()

    def greet(s, carry):
        other = lax.rem(me + s, n_all)
        pl.semaphore_signal(
            barrier,
            inc=1,
            device_id={"ops": lax.div(other, n_blk), "blk": lax.rem(other, n_blk)},
            device_id_type=MESH,
        )
        return carry

    lax.fori_loop(1, n_all, greet, 0)

    def w_copy(c):
        at = pl.ds(c * step, step)
        return pltpu.make_async_remote_copy(
            src_ref=w_send.at[at],
            dst_ref=w_recv.at[at],
            send_sem=w_ssem.at[c],
            recv_sem=w_rsem.at[c],
            device_id={"ops": ops, "blk": 1 - blk},
            device_id_type=MESH,
        )

    def wave_copy(s):
        return pltpu.make_async_remote_copy(
            src_ref=wave_ref,
            dst_ref=wave_all.at[ops],
            send_sem=wave_ssem.at[s],
            recv_sem=wave_rsem.at[s],
            device_id={"ops": lax.rem(ops + s, n_ops), "blk": blk},
            device_id_type=MESH,
        )

    near = n_ops // 2

    def out_target(s):
        side = lax.rem(lax.div(ops, near) + s // near, 2)
        return side * near + lax.rem(lax.rem(ops, near) + s % near, near)

    def out_copy(s):
        target = out_target(s)
        return pltpu.make_async_remote_copy(
            src_ref=outbox.at[pl.ds(target * capacity, capacity)],
            dst_ref=renewed_ref.at[0, pl.ds(ops * capacity, capacity)],
            send_sem=out_ssem.at[s],
            recv_sem=out_rsem.at[s],
            device_id={"ops": target, "blk": blk},
            device_id_type=MESH,
        )

    inner = sig_recv.shape[0]
    layer, place = lax.div(me, inner), lax.rem(me, inner)
    outer = sig_recv.shape[1]

    def sig_copy(s):
        other = lax.rem(place + s, inner)
        device = layer * inner + other
        return pltpu.make_async_remote_copy(
            src_ref=sig_send.at[other],
            dst_ref=sig_recv.at[place],
            send_sem=sig_ssem.at[s],
            recv_sem=sig_rsem.at[s],
            device_id={"ops": lax.div(device, n_blk), "blk": lax.rem(device, n_blk)},
            device_id_type=MESH,
        )

    def mid_copy(s):
        other = lax.rem(layer + s, outer)
        device = other * inner + place
        return pltpu.make_async_remote_copy(
            src_ref=mid_send.at[other],
            dst_ref=mid_recv.at[layer],
            send_sem=mid_ssem.at[s],
            recv_sem=mid_rsem.at[s],
            device_id={"ops": lax.div(device, n_blk), "blk": lax.rem(device, n_blk)},
            device_id_type=MESH,
        )

    rot_turned[...] = rot_ref[...].T
    rot_cols[pl.ds(0, new_half)] = rot_turned[pl.ds(blk * new_half, new_half)]
    rot_cols[pl.ds(new_half, new_half)] = rot_turned[pl.ds((1 - blk) * new_half, new_half)]
    rot_rows[pl.ds(0, half)] = rot_ref[pl.ds(blk * half, half)]
    rot_rows[pl.ds(half, half)] = rot_ref[pl.ds((1 - blk) * half, half)]

    def rotate(i, carry):
        p = 2 * i
        both = jnp.concatenate([left[p], left[p + 1]], axis=1)
        w = jnp.dot(rot_cols[...], both, preferred_element_type=jnp.float32)
        w = w.astype(jnp.bfloat16)
        w_mine[p] = w[:new_half, :half]
        w_mine[p + 1] = w[:new_half, half:]
        w_send[p] = w[new_half:, :half]
        w_send[p + 1] = w[new_half:, half:]
        return carry

    for c in range(CHUNKS):
        left_copy(c).wait()
        lax.fori_loop(c * step // 2, (c + 1) * step // 2, rotate, 0)
        if c == 0:
            pl.semaphore_wait(barrier, n_all - 1)
        else:
            w_copy(c - 1).start()

    for c in range(CHUNKS):
        right_copy(c).start()

    def start_wave(s, carry):
        wave_copy(s).start()
        return carry

    lax.fori_loop(1, n_ops, start_wave, 0)
    wave_all[ops] = wave_ref[...]
    w_copy(CHUNKS - 1).start()

    blocks[slots] = jnp.zeros(blocks.shape[1:], blocks.dtype)
    part = 4

    def renew(i, carry):
        at = pl.ds(i * part, part)
        w = jnp.concatenate(
            [
                w_mine[at].reshape(part * new_half, half),
                w_recv[at].reshape(part * new_half, half),
            ],
            axis=1,
        )
        b = jnp.dot(w, rot_rows[...], preferred_element_type=jnp.float32)
        blocks[at] = b.astype(jnp.bfloat16).reshape(part, new_half, b.shape[1])
        return carry

    for c in range(CHUNKS):
        w_copy(c).wait()
        lax.fori_loop(c * step // part, (c + 1) * step // part, renew, 0)

    def fill(s):
        first = out_target(s) * capacity
        for a in range(capacity):
            outbox[first + a] = blocks[inbox_ref[first + a]]

    last = n_ops - 1
    held = n_ops // 8
    fill(near)

    def fill_and_send(s, carry):
        fill(s + 1)
        out_copy(s).start()
        return carry

    lax.fori_loop(near, last - held, fill_and_send, 0)

    def fill_rest(s, carry):
        fill(s)
        return carry

    lax.fori_loop(last - held + 1, n_ops, fill_rest, 0)
    lax.fori_loop(0, near, fill_rest, 0)

    def wait_wave(s, carry):
        wave_copy(s).wait()
        return carry

    lax.fori_loop(1, n_ops, wait_wave, 0)
    padded = wave_all.shape[1]
    gathered = wave_all[...].reshape(n_ops * padded, wave_all.shape[2])
    columns = right_states // n_ops
    if padded == columns:
        wave_full[...] = gathered
    else:
        row = lax.broadcasted_iota(jnp.int32, (right_states, n_ops * padded), 0)
        col = lax.broadcasted_iota(jnp.int32, (right_states, n_ops * padded), 1)
        pick = (row // columns) * padded + row % columns == col
        wave_full[...] = jnp.dot(
            pick.astype(jnp.bfloat16), gathered, preferred_element_type=jnp.float32
        ).astype(jnp.bfloat16)

    own = pltpu.make_async_copy(
        outbox.at[pl.ds(ops * capacity, capacity)],
        renewed_ref.at[0, pl.ds(ops * capacity, capacity)],
        own_sem,
    )
    own.start()

    total[...] = jnp.zeros_like(total)

    def apply(g, carry):
        for q in range(GROUP):
            p = g * GROUP + q
            scale = jnp.where(p < count_ref[0], 1.0, 0.0).astype(jnp.float32)
            z = jnp.dot(right[p], wave_full[...], preferred_element_type=jnp.float32)
            z = (z * scale).astype(jnp.bfloat16)
            for n in range(vectors):
                z_group[pl.ds(n * right_states, right_states), pl.ds(q * half, half)] = z[
                    :, n * half : (n + 1) * half
                ]
        lefts = jnp.concatenate([left[g * GROUP + q] for q in range(GROUP)], axis=1)
        for n in range(vectors):
            at = pl.ds(n * right_states, right_states)
            total[at] += lax.dot_general(
                z_group[at],
                lefts,
                (((1,), (1,)), ((), ())),
                preferred_element_type=jnp.float32,
            )
        return carry

    for c in range(CHUNKS):
        right_copy(c).wait()
        lax.fori_loop(c * step // GROUP, (c + 1) * step // GROUP, apply, 0)

    rows = sigma_ref.shape[0]
    for n in range(vectors):
        at = pl.ds(n * right_states, right_states)
        turned = total[at].T.reshape(outer, inner, rows, right_states).astype(jnp.bfloat16)
        for z in range(outer):
            sig_send[:, z, :, at] = turned[z]
    sig_recv[place] = sig_send[place]

    def start_sig(s, carry):
        sig_copy(s).start()
        return carry

    def wait_sig(s, carry):
        sig_copy(s).wait()
        return carry

    lax.fori_loop(1, inner, start_sig, 0)
    lax.fori_loop(1, inner, wait_sig, 0)
    mid_send[...] = jnp.sum(sig_recv[...].astype(jnp.float32), axis=0).astype(jnp.bfloat16)
    mid_recv[layer] = mid_send[layer]

    def start_mid(s, carry):
        mid_copy(s).start()
        return carry

    def wait_mid(s, carry):
        mid_copy(s).wait()
        return carry

    lax.fori_loop(1, outer, start_mid, 0)

    def start_out(s, carry):
        out_copy(s).start()
        return carry

    lax.fori_loop(last - held, n_ops, start_out, 0)
    lax.fori_loop(1, near, start_out, 0)

    lax.fori_loop(1, outer, wait_mid, 0)
    summed = jnp.sum(mid_recv[...].astype(jnp.float32), axis=0)
    for n in range(vectors):
        sigma_ref[:, n, :] = summed[:, n * right_states : (n + 1) * right_states]

    def wait_out(s, carry):
        out_copy(s).wait()
        return carry

    lax.fori_loop(1, n_ops, wait_out, 0)
    own.wait()


def per_device(operators_left, operators_right, wavefunction, rotation, pair_count, next_owner):
    n_ops = lax.axis_size("ops")
    n_blk = lax.axis_size("blk")
    slots, left_states, half = operators_left.shape
    right_states = operators_right.shape[1]
    _, vectors, columns = wavefunction.shape
    new_states = rotation.shape[1]
    new_half = new_states // n_blk
    capacity = max(2, 2 * slots // n_ops)
    n_all = n_ops * n_blk
    rows = left_states // n_all
    inner = n_blk
    while inner * inner < n_all and n_all % (2 * inner) == 0:
        inner *= 2

    targets = next_owner[:, 0]
    number = lax.iota(jnp.int32, slots)
    living = number < pair_count[0]
    same = (targets[:, None] == targets[None, :]) & (number[None, :] < number[:, None])
    ranking = jnp.sum((same & living[None, :]).astype(jnp.int32), axis=1)
    address = jnp.where(living, targets * capacity + ranking, -1)
    hit = address[None, :] == lax.iota(jnp.int32, n_ops * capacity)[:, None]
    source = jnp.min(jnp.where(hit, number[None, :], slots), axis=1)

    padded = -(-columns // 16) * 16
    wave = wavefunction.transpose(2, 1, 0).reshape(columns, vectors * half)
    wave = jnp.pad(wave, ((0, padded - columns), (0, 0)))

    bf16 = jnp.bfloat16
    dma = pltpu.SemaphoreType.DMA
    vmem = pl.BlockSpec(memory_space=pltpu.VMEM)
    smem = pl.BlockSpec(memory_space=pltpu.SMEM)
    anywhere = pl.BlockSpec(memory_space=pl.ANY)
    return pl.pallas_call(
        functools.partial(kernel, n_ops, n_blk),
        out_shape=(
            jax.ShapeDtypeStruct((rows, vectors, right_states), jnp.float32),
            jax.ShapeDtypeStruct((1, n_ops * capacity, new_half, new_states), bf16),
        ),
        in_specs=[smem, smem, anywhere, anywhere, vmem, vmem],
        out_specs=(vmem, anywhere),
        scratch_shapes=[
            pltpu.VMEM((slots, left_states, half), bf16),
            pltpu.VMEM((slots, right_states, right_states), bf16),
            pltpu.VMEM((new_states, left_states), bf16),
            pltpu.VMEM((left_states, new_states), bf16),
            pltpu.VMEM((new_states, left_states), bf16),
            pltpu.VMEM((slots, new_half, half), bf16),
            pltpu.VMEM((slots, new_half, half), bf16),
            pltpu.VMEM((slots, new_half, half), bf16),
            pltpu.VMEM((slots + 1, new_half, new_states), bf16),
            pltpu.VMEM((n_ops * capacity, new_half, new_states), bf16),
            pltpu.VMEM((n_ops, padded, vectors * half), bf16),
            pltpu.VMEM((right_states, vectors * half), bf16),
            pltpu.VMEM((vectors * right_states, GROUP * half), bf16),
            pltpu.VMEM((vectors * right_states, left_states), jnp.float32),
            pltpu.VMEM((inner, n_all // inner, rows, vectors * right_states), bf16),
            pltpu.VMEM((inner, n_all // inner, rows, vectors * right_states), bf16),
            pltpu.VMEM((n_all // inner, rows, vectors * right_states), bf16),
            pltpu.VMEM((n_all // inner, rows, vectors * right_states), bf16),
            dma((CHUNKS,)),
            dma((CHUNKS,)),
            dma((CHUNKS,)),
            dma((CHUNKS,)),
            dma((n_ops,)),
            dma((n_ops,)),
            dma((n_ops,)),
            dma((n_ops,)),
            dma(()),
            dma((inner,)),
            dma((inner,)),
            dma((n_all // inner,)),
            dma((n_all // inner,)),
        ],
        compiler_params=pltpu.CompilerParams(collective_id=0, has_side_effects=True),
        name="davidson_step",
    )(source, pair_count, operators_left, operators_right, wave, rotation)


def solution(mesh):
    in_specs = (
        P("ops", None, "blk"),
        P("ops", None, None),
        P("blk", None, "ops"),
        P(),
        P("ops"),
        P("ops", None),
    )
    out_specs = (P(("ops", "blk"), None, None), P("ops", None, "blk", None))
    return jax.shard_map(
        per_device, mesh=mesh, in_specs=in_specs, out_specs=out_specs, check_vma=False
    )
```

```python
import functools

import jax
import jax.numpy as jnp
from jax import lax
from jax.experimental import pallas as pl
from jax.experimental.pallas import tpu as pltpu
from jax.sharding import PartitionSpec as P

MESH = pl.DeviceIdType.MESH
CHUNKS = 4
GROUP = 8


def kernel(
    n_ops,
    n_blk,
    inbox_ref,
    count_ref,
    left_hbm,
    right_hbm,
    wave_ref,
    rot_ref,
    sigma_ref,
    renewed_ref,
    left,
    right,
    rot_turned,
    rot_rows,
    rot_cols,
    w_mine,
    w_send,
    w_recv,
    blocks,
    outbox,
    wave_all,
    wave_full,
    z_group,
    total,
    sig_send,
    sig_recv,
    mid_send,
    mid_recv,
    left_sem,
    right_sem,
    w_ssem,
    w_rsem,
    wave_ssem,
    wave_rsem,
    out_ssem,
    out_rsem,
    own_sem,
    sig_ssem,
    sig_rsem,
    mid_ssem,
    mid_rsem,
):
    ops = lax.axis_index("ops")
    blk = lax.axis_index("blk")
    me = ops * n_blk + blk
    n_all = n_ops * n_blk
    slots, left_states, half = left.shape
    right_states = right.shape[1]
    new_half = w_mine.shape[1]
    vectors = sigma_ref.shape[0]
    capacity = outbox.shape[0] // n_ops
    step = slots // CHUNKS

    def left_copy(c):
        at = pl.ds(c * step, step)
        return pltpu.make_async_copy(left_hbm.at[at], left.at[at], left_sem.at[c])

    def right_copy(c):
        at = pl.ds(c * step, step)
        return pltpu.make_async_copy(right_hbm.at[at], right.at[at], right_sem.at[c])

    for c in range(CHUNKS):
        left_copy(c).start()
    barrier = pltpu.get_barrier_semaphore()

    def greet(s, carry):
        other = lax.rem(me + s, n_all)
        pl.semaphore_signal(
            barrier,
            inc=1,
            device_id={"ops": lax.div(other, n_blk), "blk": lax.rem(other, n_blk)},
            device_id_type=MESH,
        )
        return carry

    lax.fori_loop(1, n_all, greet, 0)

    def w_copy(c):
        at = pl.ds(c * step, step)
        return pltpu.make_async_remote_copy(
            src_ref=w_send.at[at],
            dst_ref=w_recv.at[at],
            send_sem=w_ssem.at[c],
            recv_sem=w_rsem.at[c],
            device_id={"ops": ops, "blk": 1 - blk},
            device_id_type=MESH,
        )

    def wave_copy(s):
        return pltpu.make_async_remote_copy(
            src_ref=wave_ref,
            dst_ref=wave_all.at[ops],
            send_sem=wave_ssem.at[s],
            recv_sem=wave_rsem.at[s],
            device_id={"ops": lax.rem(ops + s, n_ops), "blk": blk},
            device_id_type=MESH,
        )

    near = n_ops // 2

    def out_target(s):
        side = lax.rem(lax.div(ops, near) + s // near, 2)
        return side * near + lax.rem(lax.rem(ops, near) + s % near, near)

    def out_copy(s):
        target = out_target(s)
        return pltpu.make_async_remote_copy(
            src_ref=outbox.at[pl.ds(target * capacity, capacity)],
            dst_ref=renewed_ref.at[0, pl.ds(ops * capacity, capacity)],
            send_sem=out_ssem.at[s],
            recv_sem=out_rsem.at[s],
            device_id={"ops": target, "blk": blk},
            device_id_type=MESH,
        )

    inner = sig_recv.shape[0]
    layer, place = lax.div(me, inner), lax.rem(me, inner)
    outer = sig_recv.shape[1]

    def sig_copy(s):
        other = lax.rem(place + s, inner)
        device = layer * inner + other
        return pltpu.make_async_remote_copy(
            src_ref=sig_send.at[other],
            dst_ref=sig_recv.at[place],
            send_sem=sig_ssem.at[s],
            recv_sem=sig_rsem.at[s],
            device_id={"ops": lax.div(device, n_blk), "blk": lax.rem(device, n_blk)},
            device_id_type=MESH,
        )

    def mid_copy(s):
        other = lax.rem(layer + s, outer)
        device = other * inner + place
        return pltpu.make_async_remote_copy(
            src_ref=mid_send.at[other],
            dst_ref=mid_recv.at[layer],
            send_sem=mid_ssem.at[s],
            recv_sem=mid_rsem.at[s],
            device_id={"ops": lax.div(device, n_blk), "blk": lax.rem(device, n_blk)},
            device_id_type=MESH,
        )

    rot_turned[...] = rot_ref[...].T
    rot_cols[pl.ds(0, new_half)] = rot_turned[pl.ds(blk * new_half, new_half)]
    rot_cols[pl.ds(new_half, new_half)] = rot_turned[pl.ds((1 - blk) * new_half, new_half)]
    rot_rows[pl.ds(0, half)] = rot_ref[pl.ds(blk * half, half)]
    rot_rows[pl.ds(half, half)] = rot_ref[pl.ds((1 - blk) * half, half)]

    def rotate(i, carry):
        turned = rot_cols[...]
        for q in range(0, GROUP, 2):
            p = GROUP * i + q
            both = jnp.concatenate([left[p], left[p + 1]], axis=1)
            w = jnp.dot(turned, both, preferred_element_type=jnp.float32)
            w = w.astype(jnp.bfloat16)
            w_mine[p] = w[:new_half, :half]
            w_mine[p + 1] = w[:new_half, half:]
            w_send[p] = w[new_half:, :half]
            w_send[p + 1] = w[new_half:, half:]
        return carry

    for c in range(CHUNKS):
        left_copy(c).wait()
        lax.fori_loop(c * step // GROUP, (c + 1) * step // GROUP, rotate, 0)
        if c == 0:
            pl.semaphore_wait(barrier, n_all - 1)
        else:
            w_copy(c - 1).start()

    for c in range(CHUNKS):
        right_copy(c).start()

    def start_wave(s, carry):
        wave_copy(s).start()
        return carry

    lax.fori_loop(1, n_ops, start_wave, 0)
    wave_all[ops] = wave_ref[...]
    w_copy(CHUNKS - 1).start()

    blocks[slots] = jnp.zeros(blocks.shape[1:], blocks.dtype)
    part = step

    def renew(i, carry):
        at = pl.ds(i * part, part)
        w = jnp.concatenate(
            [
                w_mine[at].reshape(part * new_half, half),
                w_recv[at].reshape(part * new_half, half),
            ],
            axis=1,
        )
        b = jnp.dot(w, rot_rows[...], preferred_element_type=jnp.float32)
        blocks[at] = b.astype(jnp.bfloat16).reshape(part, new_half, b.shape[1])
        return carry

    for c in range(CHUNKS):
        w_copy(c).wait()
        lax.fori_loop(c * step // part, (c + 1) * step // part, renew, 0)

    def fill(s):
        first = out_target(s) * capacity
        for a in range(capacity):
            outbox[first + a] = blocks[inbox_ref[first + a]]

    def turn(t):
        return 1 + lax.rem(t + near - 1, n_ops - 1)

    fill(near)

    def fill_and_send(t, carry):
        fill(turn(t + 1))
        out_copy(turn(t)).start()
        return carry

    lax.fori_loop(0, n_ops - 2, fill_and_send, 0)
    fill(0)
    out_copy(near - 1).start()

    def wait_wave(s, carry):
        wave_copy(s).wait()
        return carry

    lax.fori_loop(1, n_ops, wait_wave, 0)
    padded = wave_all.shape[1]
    gathered = wave_all[...].reshape(n_ops * padded, wave_all.shape[2])
    columns = right_states // n_ops
    if padded == columns:
        wave_full[...] = gathered
    else:
        row = lax.broadcasted_iota(jnp.int32, (right_states, n_ops * padded), 0)
        col = lax.broadcasted_iota(jnp.int32, (right_states, n_ops * padded), 1)
        pick = (row // columns) * padded + row % columns == col
        wave_full[...] = jnp.dot(
            pick.astype(jnp.bfloat16), gathered, preferred_element_type=jnp.float32
        ).astype(jnp.bfloat16)

    own = pltpu.make_async_copy(
        outbox.at[pl.ds(ops * capacity, capacity)],
        renewed_ref.at[0, pl.ds(ops * capacity, capacity)],
        own_sem,
    )
    own.start()

    total[...] = jnp.zeros_like(total)

    def apply(g, carry):
        for q in range(GROUP):
            p = g * GROUP + q
            scale = jnp.where(p < count_ref[0], 1.0, 0.0).astype(jnp.float32)
            z = jnp.dot(right[p], wave_full[...], preferred_element_type=jnp.float32)
            z = (z * scale).astype(jnp.bfloat16)
            for n in range(vectors):
                z_group[pl.ds(n * right_states, right_states), pl.ds(q * half, half)] = z[
                    :, n * half : (n + 1) * half
                ]
        lefts = jnp.concatenate([left[g * GROUP + q] for q in range(GROUP)], axis=1)
        for n in range(vectors):
            at = pl.ds(n * right_states, right_states)
            total[at] += lax.dot_general(
                z_group[at],
                lefts,
                (((1,), (1,)), ((), ())),
                preferred_element_type=jnp.float32,
            )
        return carry

    for c in range(CHUNKS):
        right_copy(c).wait()
        lax.fori_loop(c * step // GROUP, (c + 1) * step // GROUP, apply, 0)

    rows = sigma_ref.shape[1]
    for n in range(vectors):
        at = pl.ds(n * right_states, right_states)
        turned = total[at].T.reshape(outer, inner, rows, right_states).astype(jnp.bfloat16)
        for z in range(outer):
            sig_send[:, z, :, at] = turned[z]
    sig_recv[place] = sig_send[place]

    def start_sig(s, carry):
        sig_copy(s).start()
        return carry

    def wait_sig(s, carry):
        sig_copy(s).wait()
        return carry

    lax.fori_loop(1, inner, start_sig, 0)
    lax.fori_loop(1, inner, wait_sig, 0)
    mid_send[...] = jnp.sum(sig_recv[...].astype(jnp.float32), axis=0).astype(jnp.bfloat16)
    mid_recv[layer] = mid_send[layer]

    def start_mid(s, carry):
        mid_copy(s).start()
        return carry

    def wait_mid(s, carry):
        mid_copy(s).wait()
        return carry

    lax.fori_loop(1, outer, start_mid, 0)

    lax.fori_loop(1, outer, wait_mid, 0)
    summed = jnp.sum(mid_recv[...].astype(jnp.float32), axis=0)
    for n in range(vectors):
        sigma_ref[n] = summed[:, n * right_states : (n + 1) * right_states]

    def wait_out(s, carry):
        out_copy(s).wait()
        return carry

    lax.fori_loop(1, n_ops, wait_out, 0)
    own.wait()


def per_device(operators_left, operators_right, wavefunction, rotation, pair_count, next_owner):
    n_ops = lax.axis_size("ops")
    n_blk = lax.axis_size("blk")
    slots, left_states, half = operators_left.shape
    right_states = operators_right.shape[1]
    _, vectors, columns = wavefunction.shape
    new_states = rotation.shape[1]
    new_half = new_states // n_blk
    capacity = max(2, 2 * slots // n_ops)
    n_all = n_ops * n_blk
    rows = left_states // n_all
    inner = n_blk
    while inner * inner < n_all and n_all % (2 * inner) == 0:
        inner *= 2

    targets = next_owner[:, 0]
    number = lax.iota(jnp.int32, slots)
    living = number < pair_count[0]
    same = (targets[:, None] == targets[None, :]) & (number[None, :] < number[:, None])
    ranking = jnp.sum((same & living[None, :]).astype(jnp.int32), axis=1)
    address = jnp.where(living, targets * capacity + ranking, -1)
    hit = address[None, :] == lax.iota(jnp.int32, n_ops * capacity)[:, None]
    source = jnp.min(jnp.where(hit, number[None, :], slots), axis=1)

    padded = -(-columns // 16) * 16
    wave = wavefunction.transpose(2, 1, 0).reshape(columns, vectors * half)
    wave = jnp.pad(wave, ((0, padded - columns), (0, 0)))

    bf16 = jnp.bfloat16
    dma = pltpu.SemaphoreType.DMA
    vmem = pl.BlockSpec(memory_space=pltpu.VMEM)
    smem = pl.BlockSpec(memory_space=pltpu.SMEM)
    anywhere = pl.BlockSpec(memory_space=pl.ANY)
    sigma, renewed = pl.pallas_call(
        functools.partial(kernel, n_ops, n_blk),
        out_shape=(
            jax.ShapeDtypeStruct((vectors, rows, right_states), jnp.float32),
            jax.ShapeDtypeStruct((1, n_ops * capacity, new_half, new_states), bf16),
        ),
        in_specs=[smem, smem, anywhere, anywhere, vmem, vmem],
        out_specs=(vmem, anywhere),
        scratch_shapes=[
            pltpu.VMEM((slots, left_states, half), bf16),
            pltpu.VMEM((slots, right_states, right_states), bf16),
            pltpu.VMEM((new_states, left_states), bf16),
            pltpu.VMEM((left_states, new_states), bf16),
            pltpu.VMEM((new_states, left_states), bf16),
            pltpu.VMEM((slots, new_half, half), bf16),
            pltpu.VMEM((slots, new_half, half), bf16),
            pltpu.VMEM((slots, new_half, half), bf16),
            pltpu.VMEM((slots + 1, new_half, new_states), bf16),
            pltpu.VMEM((n_ops * capacity, new_half, new_states), bf16),
            pltpu.VMEM((n_ops, padded, vectors * half), bf16),
            pltpu.VMEM((right_states, vectors * half), bf16),
            pltpu.VMEM((vectors * right_states, GROUP * half), bf16),
            pltpu.VMEM((vectors * right_states, left_states), jnp.float32),
            pltpu.VMEM((inner, n_all // inner, rows, vectors * right_states), bf16),
            pltpu.VMEM((inner, n_all // inner, rows, vectors * right_states), bf16),
            pltpu.VMEM((n_all // inner, rows, vectors * right_states), bf16),
            pltpu.VMEM((n_all // inner, rows, vectors * right_states), bf16),
            dma((CHUNKS,)),
            dma((CHUNKS,)),
            dma((CHUNKS,)),
            dma((CHUNKS,)),
            dma((n_ops,)),
            dma((n_ops,)),
            dma((n_ops,)),
            dma((n_ops,)),
            dma(()),
            dma((inner,)),
            dma((inner,)),
            dma((n_all // inner,)),
            dma((n_all // inner,)),
        ],
        compiler_params=pltpu.CompilerParams(collective_id=0, has_side_effects=True),
        name="davidson_step",
    )(source, pair_count, operators_left, operators_right, wave, rotation)
    return sigma.transpose(1, 0, 2), renewed


def solution(mesh):
    in_specs = (
        P("ops", None, "blk"),
        P("ops", None, None),
        P("blk", None, "ops"),
        P(),
        P("ops"),
        P("ops", None),
    )
    out_specs = (P(("ops", "blk"), None, None), P("ops", None, "blk", None))
    return jax.shard_map(
        per_device, mesh=mesh, in_specs=in_specs, out_specs=out_specs, check_vma=False
    )
```

```python
import functools

import jax
import jax.numpy as jnp
from jax import lax
from jax.experimental import pallas as pl
from jax.experimental.pallas import tpu as pltpu
from jax.sharding import PartitionSpec as P

MESH = pl.DeviceIdType.MESH
CHUNKS = 4
GROUP = 8


def kernel(
    n_ops,
    n_blk,
    inbox_ref,
    count_ref,
    left_hbm,
    right_hbm,
    wave_ref,
    rot_ref,
    sigma_ref,
    renewed_ref,
    left,
    right,
    rot_turned,
    rot_rows,
    rot_cols,
    w_mine,
    w_send,
    w_recv,
    blocks,
    outbox,
    wave_all,
    wave_full,
    z_group,
    total,
    sig_send,
    sig_recv,
    mid_send,
    mid_recv,
    left_sem,
    right_sem,
    w_ssem,
    w_rsem,
    wave_ssem,
    wave_rsem,
    out_ssem,
    out_rsem,
    own_sem,
    sig_ssem,
    sig_rsem,
    mid_ssem,
    mid_rsem,
):
    ops = lax.axis_index("ops")
    blk = lax.axis_index("blk")
    me = ops * n_blk + blk
    n_all = n_ops * n_blk
    slots, left_states, half = left.shape
    right_states = right.shape[1]
    new_half = w_mine.shape[1]
    vectors = sigma_ref.shape[0]
    capacity = outbox.shape[0] // n_ops
    step = slots // CHUNKS

    def left_copy(c):
        at = pl.ds(c * step, step)
        return pltpu.make_async_copy(left_hbm.at[at], left.at[at], left_sem.at[c])

    def right_copy(c):
        at = pl.ds(c * step, step)
        return pltpu.make_async_copy(right_hbm.at[at], right.at[at], right_sem.at[c])

    for c in range(CHUNKS):
        left_copy(c).start()
    barrier = pltpu.get_barrier_semaphore()

    def greet(s, carry):
        other = lax.rem(me + s, n_all)
        pl.semaphore_signal(
            barrier,
            inc=1,
            device_id={"ops": lax.div(other, n_blk), "blk": lax.rem(other, n_blk)},
            device_id_type=MESH,
        )
        return carry

    lax.fori_loop(1, n_all, greet, 0)

    def w_copy(c):
        at = pl.ds(c * step, step)
        return pltpu.make_async_remote_copy(
            src_ref=w_send.at[at],
            dst_ref=w_recv.at[at],
            send_sem=w_ssem.at[c],
            recv_sem=w_rsem.at[c],
            device_id={"ops": ops, "blk": 1 - blk},
            device_id_type=MESH,
        )

    def wave_copy(s):
        return pltpu.make_async_remote_copy(
            src_ref=wave_ref,
            dst_ref=wave_all.at[ops],
            send_sem=wave_ssem.at[s],
            recv_sem=wave_rsem.at[s],
            device_id={"ops": lax.rem(ops + s, n_ops), "blk": blk},
            device_id_type=MESH,
        )

    near = n_ops // 2

    def out_target(s):
        side = lax.rem(lax.div(ops, near) + s // near, 2)
        return side * near + lax.rem(lax.rem(ops, near) + s % near, near)

    def out_copy(s):
        target = out_target(s)
        return pltpu.make_async_remote_copy(
            src_ref=outbox.at[pl.ds(target * capacity, capacity)],
            dst_ref=renewed_ref.at[0, pl.ds(ops * capacity, capacity)],
            send_sem=out_ssem.at[s],
            recv_sem=out_rsem.at[s],
            device_id={"ops": target, "blk": blk},
            device_id_type=MESH,
        )

    inner = sig_recv.shape[0]
    layer, place = lax.div(me, inner), lax.rem(me, inner)
    outer = sig_recv.shape[1]

    def sig_copy(s):
        other = lax.rem(place + s, inner)
        device = layer * inner + other
        return pltpu.make_async_remote_copy(
            src_ref=sig_send.at[other],
            dst_ref=sig_recv.at[place],
            send_sem=sig_ssem.at[s],
            recv_sem=sig_rsem.at[s],
            device_id={"ops": lax.div(device, n_blk), "blk": lax.rem(device, n_blk)},
            device_id_type=MESH,
        )

    def mid_copy(s):
        other = lax.rem(layer + s, outer)
        device = other * inner + place
        return pltpu.make_async_remote_copy(
            src_ref=mid_send.at[other],
            dst_ref=mid_recv.at[layer],
            send_sem=mid_ssem.at[s],
            recv_sem=mid_rsem.at[s],
            device_id={"ops": lax.div(device, n_blk), "blk": lax.rem(device, n_blk)},
            device_id_type=MESH,
        )

    rot_turned[...] = rot_ref[...].T
    rot_cols[pl.ds(0, new_half)] = rot_turned[pl.ds(blk * new_half, new_half)]
    rot_cols[pl.ds(new_half, new_half)] = rot_turned[pl.ds((1 - blk) * new_half, new_half)]
    rot_rows[pl.ds(0, half)] = rot_ref[pl.ds(blk * half, half)]
    rot_rows[pl.ds(half, half)] = rot_ref[pl.ds((1 - blk) * half, half)]

    def rotate(i, carry):
        turned = rot_cols[...]
        for q in range(0, GROUP, 2):
            p = GROUP * i + q
            both = jnp.concatenate([left[p], left[p + 1]], axis=1)
            w = jnp.dot(turned, both, preferred_element_type=jnp.float32)
            w = w.astype(jnp.bfloat16)
            w_mine[p] = w[:new_half, :half]
            w_mine[p + 1] = w[:new_half, half:]
            w_send[p] = w[new_half:, :half]
            w_send[p + 1] = w[new_half:, half:]
        return carry

    for c in range(CHUNKS):
        left_copy(c).wait()
        lax.fori_loop(c * step // GROUP, (c + 1) * step // GROUP, rotate, 0)
        if c == 0:
            pl.semaphore_wait(barrier, n_all - 1)
        else:
            w_copy(c - 1).start()

    for c in range(CHUNKS):
        right_copy(c).start()

    def start_wave(s, carry):
        wave_copy(s).start()
        return carry

    lax.fori_loop(1, n_ops, start_wave, 0)
    wave_all[ops] = wave_ref[...]
    w_copy(CHUNKS - 1).start()

    blocks[slots] = jnp.zeros(blocks.shape[1:], blocks.dtype)
    part = step

    def renew(i, carry):
        at = pl.ds(i * part, part)
        w = jnp.concatenate(
            [
                w_mine[at].reshape(part * new_half, half),
                w_recv[at].reshape(part * new_half, half),
            ],
            axis=1,
        )
        b = jnp.dot(w, rot_rows[...], preferred_element_type=jnp.float32)
        blocks[at] = b.astype(jnp.bfloat16).reshape(part, new_half, b.shape[1])
        return carry

    for c in range(CHUNKS):
        w_copy(c).wait()
        lax.fori_loop(c * step // part, (c + 1) * step // part, renew, 0)

    def fill(s):
        first = out_target(s) * capacity
        for a in range(capacity):
            outbox[first + a] = blocks[inbox_ref[first + a]]

    def turn(t):
        return 1 + lax.rem(t + near - 1, n_ops - 1)

    fill(near)

    def fill_and_send(t, carry):
        fill(turn(t + 1))
        out_copy(turn(t)).start()
        return carry

    lax.fori_loop(0, n_ops - 2, fill_and_send, 0)
    fill(0)
    out_copy(near - 1).start()

    def wait_wave(s, carry):
        wave_copy(s).wait()
        return carry

    lax.fori_loop(1, n_ops, wait_wave, 0)
    padded = wave_all.shape[1]
    gathered = wave_all[...].reshape(n_ops * padded, wave_all.shape[2])
    columns = right_states // n_ops
    if padded == columns:
        wave_full[...] = gathered
    else:
        row = lax.broadcasted_iota(jnp.int32, (right_states, n_ops * padded), 0)
        col = lax.broadcasted_iota(jnp.int32, (right_states, n_ops * padded), 1)
        pick = (row // columns) * padded + row % columns == col
        wave_full[...] = jnp.dot(
            pick.astype(jnp.bfloat16), gathered, preferred_element_type=jnp.float32
        ).astype(jnp.bfloat16)

    own = pltpu.make_async_copy(
        outbox.at[pl.ds(ops * capacity, capacity)],
        renewed_ref.at[0, pl.ds(ops * capacity, capacity)],
        own_sem,
    )
    own.start()

    total[...] = jnp.zeros_like(total)

    def apply(g, carry):
        for q in range(GROUP):
            p = g * GROUP + q
            scale = jnp.where(p < count_ref[0], 1.0, 0.0).astype(jnp.float32)
            z = jnp.dot(right[p], wave_full[...], preferred_element_type=jnp.float32)
            z = (z * scale).astype(jnp.bfloat16)
            for n in range(vectors):
                z_group[pl.ds(n * right_states, right_states), pl.ds(q * half, half)] = z[
                    :, n * half : (n + 1) * half
                ]
        lefts = jnp.concatenate([left[g * GROUP + q] for q in range(GROUP)], axis=1)
        for n in range(vectors):
            at = pl.ds(n * right_states, right_states)
            total[at] += lax.dot_general(
                z_group[at],
                lefts,
                (((1,), (1,)), ((), ())),
                preferred_element_type=jnp.float32,
            )
        return carry

    for c in range(CHUNKS):
        right_copy(c).wait()
        lax.fori_loop(c * step // GROUP, (c + 1) * step // GROUP, apply, 0)

    rows = sigma_ref.shape[1]
    for n in range(vectors):
        at = pl.ds(n * right_states, right_states)
        turned = total[at].T.reshape(outer, inner, rows, right_states).astype(jnp.bfloat16)
        for z in range(outer):
            sig_send[:, z, :, at] = turned[z]
    sig_recv[place] = sig_send[place]

    def start_sig(s, carry):
        sig_copy(s).start()
        return carry

    def wait_sig(s, carry):
        sig_copy(s).wait()
        return carry

    lax.fori_loop(1, inner, start_sig, 0)
    lax.fori_loop(1, inner, wait_sig, 0)
    mid_send[...] = jnp.sum(sig_recv[...].astype(jnp.float32), axis=0).astype(jnp.bfloat16)
    mid_recv[layer] = mid_send[layer]

    def start_mid(s, carry):
        mid_copy(s).start()
        return carry

    def wait_mid(s, carry):
        mid_copy(s).wait()
        return carry

    lax.fori_loop(1, outer, start_mid, 0)

    lax.fori_loop(1, outer, wait_mid, 0)
    summed = jnp.sum(mid_recv[...].astype(jnp.float32), axis=0)
    for n in range(vectors):
        sigma_ref[n] = summed[:, n * right_states : (n + 1) * right_states]

    def wait_out(s, carry):
        out_copy(s).wait()
        return carry

    lax.fori_loop(1, n_ops, wait_out, 0)
    own.wait()


def per_device(operators_left, operators_right, wavefunction, rotation, pair_count, next_owner):
    n_ops = lax.axis_size("ops")
    n_blk = lax.axis_size("blk")
    slots, left_states, half = operators_left.shape
    right_states = operators_right.shape[1]
    _, vectors, columns = wavefunction.shape
    new_states = rotation.shape[1]
    new_half = new_states // n_blk
    capacity = max(2, 2 * slots // n_ops)
    n_all = n_ops * n_blk
    rows = left_states // n_all
    inner = n_blk
    while inner * inner < n_all and n_all % (2 * inner) == 0:
        inner *= 2

    targets = next_owner[:, 0]
    number = lax.iota(jnp.int32, slots)
    living = number < pair_count[0]
    same = (targets[:, None] == targets[None, :]) & (number[None, :] < number[:, None])
    ranking = jnp.sum((same & living[None, :]).astype(jnp.int32), axis=1)
    address = jnp.where(living, targets * capacity + ranking, -1)
    hit = address[None, :] == lax.iota(jnp.int32, n_ops * capacity)[:, None]
    source = jnp.min(jnp.where(hit, number[None, :], slots), axis=1)

    padded = -(-columns // 16) * 16
    wave = wavefunction.transpose(2, 1, 0).reshape(columns, vectors * half)
    wave = jnp.pad(wave, ((0, padded - columns), (0, 0)))

    bf16 = jnp.bfloat16
    dma = pltpu.SemaphoreType.DMA
    vmem = pl.BlockSpec(memory_space=pltpu.VMEM)
    smem = pl.BlockSpec(memory_space=pltpu.SMEM)
    anywhere = pl.BlockSpec(memory_space=pl.ANY)
    sigma, renewed = pl.pallas_call(
        functools.partial(kernel, n_ops, n_blk),
        out_shape=(
            jax.ShapeDtypeStruct((vectors, rows, right_states), jnp.float32),
            pltpu.VMEM((1, n_ops * capacity, new_half, new_states), bf16),
        ),
        in_specs=[smem, smem, anywhere, anywhere, vmem, vmem],
        out_specs=(vmem, vmem),
        scratch_shapes=[
            pltpu.VMEM((slots, left_states, half), bf16),
            pltpu.VMEM((slots, right_states, right_states), bf16),
            pltpu.VMEM((new_states, left_states), bf16),
            pltpu.VMEM((left_states, new_states), bf16),
            pltpu.VMEM((new_states, left_states), bf16),
            pltpu.VMEM((slots, new_half, half), bf16),
            pltpu.VMEM((slots, new_half, half), bf16),
            pltpu.VMEM((slots, new_half, half), bf16),
            pltpu.VMEM((slots + 1, new_half, new_states), bf16),
            pltpu.VMEM((n_ops * capacity, new_half, new_states), bf16),
            pltpu.VMEM((n_ops, padded, vectors * half), bf16),
            pltpu.VMEM((right_states, vectors * half), bf16),
            pltpu.VMEM((vectors * right_states, GROUP * half), bf16),
            pltpu.VMEM((vectors * right_states, left_states), jnp.float32),
            pltpu.VMEM((inner, n_all // inner, rows, vectors * right_states), bf16),
            pltpu.VMEM((inner, n_all // inner, rows, vectors * right_states), bf16),
            pltpu.VMEM((n_all // inner, rows, vectors * right_states), bf16),
            pltpu.VMEM((n_all // inner, rows, vectors * right_states), bf16),
            dma((CHUNKS,)),
            dma((CHUNKS,)),
            dma((CHUNKS,)),
            dma((CHUNKS,)),
            dma((n_ops,)),
            dma((n_ops,)),
            dma((n_ops,)),
            dma((n_ops,)),
            dma(()),
            dma((inner,)),
            dma((inner,)),
            dma((n_all // inner,)),
            dma((n_all // inner,)),
        ],
        compiler_params=pltpu.CompilerParams(collective_id=0, has_side_effects=True),
        name="davidson_step",
    )(source, pair_count, operators_left, operators_right, wave, rotation)
    return sigma.transpose(1, 0, 2), renewed


def solution(mesh):
    in_specs = (
        P("ops", None, "blk"),
        P("ops", None, None),
        P("blk", None, "ops"),
        P(),
        P("ops"),
        P("ops", None),
    )
    out_specs = (P(("ops", "blk"), None, None), P("ops", None, "blk", None))
    return jax.shard_map(
        per_device, mesh=mesh, in_specs=in_specs, out_specs=out_specs, check_vma=False
    )
```
